128 devices in a mesh: rep: 4 (over z_lo, core), ep: 32 (over y, x, z_hi).
Axes of the slice: x: 4, y: 4, z: 4 (z_hi: 2, z_lo: 2; z = z_hi * 2 + z_lo), core: 2. Of those that a mesh axis runs over, the one named last changes fastest.
Arguments:
- tokens: bfloat16 [16384, 2048], P(('rep', 'ep')), may hold values from -6 to 6
- expert_ids: int32 [16384, 8], P(('rep', 'ep')), may hold values from 0 to 127, as said below
- route_weight: float32 [16384, 8], P(('rep', 'ep')), may hold values from 0.05 to 1
- hot_plan: int32 [32], replicated, may hold values from 0 to 3, as said below
- gate_proj: bfloat16 [128, 2048, 768], P(('rep', 'ep')), may hold values from -0.125 to 0.125
- up_proj: bfloat16 [128, 2048, 768], P(('rep', 'ep')), may hold values from -0.125 to 0.125
- down_proj: bfloat16 [128, 768, 2048], P(('rep', 'ep')), may hold values from -0.21875 to 0.21875
Outputs:
- layer_out: bfloat16 [16384, 2048], P(('rep', 'ep'))
- served_load: float32 [128], replicated
The draws below stay inside these ranges and needn't reach their ends.
Inputs may be any that keep to these rules, and one draw needn't show every extreme that they name: `expert_ids`: within the rows of one device (aligned blocks of 128 tokens) a hot expert is named at most 16 times and any other expert at most 6 times. Some expert that is not hot is named exactly 6 times in every block, and the hot expert of some column exactly 16 times in every block. Expert hot_plan[c] * 32 + c is the hot expert of column c.
All inputs are finite; a program needn't handle non-finite values.
Results may differ from the reference program's by a relative error of at most 0.0057.
Values may be sent and summed in bfloat16 or wider, within the bound.
No kernel may reach another device: no remote copies, remote signals or barrier semaphores. Data moves between devices by JAX's collectives and lax.ppermute only.
A program may use at most 128 MiB of HBM per device.

```python
import math
import jax
import jax.numpy as jnp
from jax import lax

D = 2048
FF = 768
TOPK = 8
TOK_DEV = 128
EXPERTS = 128
HOT = 32
TOKENS = 16384
CAP = 6
HOT_CAP = 16


def plan_rows(key):
    return jax.random.randint(jax.random.fold_in(key, 11), (HOT,), 0, EXPERTS // HOT).astype(jnp.int32)


def draw_hot_plan(key, part):
    return plan_rows(key)


def draw_expert_ids(key, part):
    hot_rows = plan_rows(key)
    expert_range = jnp.arange(EXPERTS, dtype=jnp.int32)
    hot_flag = expert_range // HOT == hot_rows[expert_range % HOT]
    maxima = jnp.where(hot_flag, HOT_CAP, CAP).astype(jnp.int32)
    total_units = (EXPERTS - HOT) * CAP + HOT * HOT_CAP
    routed = TOK_DEV * TOPK
    removed = total_units - routed
    unit_expert = jnp.repeat(expert_range, maxima, total_repeat_length=total_units).astype(jnp.int32)
    cool_list = jnp.nonzero(jnp.logical_not(hot_flag), size=EXPERTS - HOT, fill_value=0)[0].astype(jnp.int32)
    cool_pick = cool_list[jax.random.randint(jax.random.fold_in(key, 12), (), 0, EXPERTS - HOT)]
    hot_column = jax.random.randint(jax.random.fold_in(key, 13), (), 0, HOT)
    hot_pick = hot_rows[hot_column] * HOT + hot_column
    protected = (unit_expert == cool_pick) | (unit_expert == hot_pick)
    score_span = (2 ** 31 - 1) // total_units - 1
    half_span = score_span // 2
    unit_range = jnp.arange(total_units, dtype=jnp.int32)
    row_favour = jax.random.randint(jax.random.fold_in(key, 15), (EXPERTS // HOT, EXPERTS), 0, 8) == 0

    def one_device(index):
        dev_key = jax.random.fold_in(jax.random.fold_in(key, 14), index)
        row_index = index // HOT
        favoured = row_favour[row_index][unit_expert]
        raw_scores = jax.random.randint(jax.random.fold_in(dev_key, 1), (total_units,), 0, half_span)
        raw_scores = raw_scores + jnp.where(favoured, 0, half_span).astype(jnp.int32)
        scores = raw_scores * total_units + unit_range
        scores = jnp.where(protected, score_span * total_units + unit_range, scores)
        removal_order = jnp.argsort(scores, stable=True)
        kept_mask = jnp.ones((total_units,), jnp.bool_).at[removal_order[:removed]].set(False)
        kept_idx = jnp.nonzero(kept_mask, size=routed, fill_value=0)[0]
        id_table = unit_expert[kept_idx].reshape(TOPK, TOK_DEV).T
        token_perm = jax.random.permutation(jax.random.fold_in(dev_key, 2), TOK_DEV)
        id_table = id_table[token_perm]
        slot_scores = jax.random.randint(jax.random.fold_in(dev_key, 3), (TOK_DEV, TOPK), 0, 2 ** 20) * TOPK + jnp.arange(TOPK, dtype=jnp.int32)[None, :]
        slot_order = jnp.argsort(slot_scores, axis=1, stable=True)
        return jnp.take_along_axis(id_table, slot_order, axis=1)
    device_range = jnp.arange(TOKENS // TOK_DEV, dtype=jnp.int32)
    return jax.vmap(one_device)(device_range).reshape(TOKENS, TOPK).astype(jnp.int32)


def shard_levels(own_key, shape, cuts, least, high):
    def one(axis_at, blocks):
        heights = jax.random.uniform(jax.random.fold_in(jax.random.fold_in(own_key, 6), axis_at), (blocks,), jnp.float32, least / len(cuts), high / len(cuts))
        return jnp.repeat(jnp.exp(heights), shape[axis_at] // blocks).reshape((-1,) + (1,) * (len(shape) - axis_at - 1))

    loudness = one(*cuts[0])
    for cut in cuts[1:]:
        loudness = loudness * one(*cut)
    return loudness


def noise(stream_key, dims, width, reach, shards=(), kind=jnp.bfloat16):
    values = width * jax.random.normal(stream_key, dims, jnp.float32)
    if shards:
        values = values * shard_levels(stream_key, dims, shards, -0.22, 0.18)
    return jnp.clip(values, -reach, reach).astype(kind)


def setup_inputs(seed: int = 0) -> dict:
    streams_of = jax.random.split(jax.random.key(seed), 8)
    tokens = noise(streams_of[0], (TOKENS, D), 1.0, 6.0, ((0, 128),))
    expert_ids = draw_expert_ids(jax.random.fold_in(streams_of[7], 71), 0)
    route_weight = jnp.clip(jnp.exp(math.log(1.0) - 2.9957323 * jax.random.uniform(streams_of[2], (TOKENS, TOPK), jnp.float32) ** shard_levels(streams_of[2], (TOKENS, TOPK), ((0, 128),), -0.2, 0.2)), 0.05, 1.0)
    hot_plan = draw_hot_plan(jax.random.fold_in(streams_of[7], 71), 0)
    gate_proj = noise(streams_of[4], (EXPERTS, D, FF), D ** -0.5, 0.125, ((0, 128),))
    up_proj = noise(streams_of[5], (EXPERTS, D, FF), D ** -0.5, 0.125, ((0, 128),))
    down_proj = noise(streams_of[6], (EXPERTS, FF, D), FF ** -0.5, 0.21875, ((0, 128),))
    return {"tokens": tokens, "expert_ids": expert_ids, "route_weight": route_weight, "hot_plan": hot_plan, "gate_proj": gate_proj, "up_proj": up_proj, "down_proj": down_proj}


def reference(tokens, expert_ids, route_weight, hot_plan, gate_proj, up_proj, down_proj):
    flat_ids = expert_ids.reshape(-1)
    routed = flat_ids.shape[0]
    experts = gate_proj.shape[0]
    devices = tokens.shape[0] // TOK_DEV
    expert_range = jnp.arange(experts, dtype=jnp.int32)
    hot_flag = (expert_range // HOT) == hot_plan[expert_range % HOT]
    row_ids = flat_ids.reshape(experts // HOT, -1)

    def count_row(ids):
        return jnp.sum((ids[:, None] == expert_range[None, :]).astype(jnp.int32), axis=0, dtype=jnp.int32)

    row_counts = lax.map(count_row, row_ids)
    counts = jnp.sum(row_counts, axis=0, dtype=jnp.int32)
    hot_expert = (hot_plan * HOT + jnp.arange(HOT, dtype=jnp.int32)).astype(jnp.int32)
    copy_rows = row_counts[:, hot_expert].reshape(-1)
    served = jnp.where(hot_flag, jnp.zeros_like(counts), counts) + copy_rows
    served_load = served.astype(jnp.float32) / jnp.float32(TOK_DEV * TOPK)

    shares = route_weight / jnp.sum(route_weight, axis=1, keepdims=True)
    flat_shares = shares.reshape(-1)

    def make_step(bound_rows):
        def one_expert(summed, expert):
            picked = jnp.nonzero(flat_ids == expert, size=bound_rows, fill_value=routed)[0].astype(jnp.int32)
            living = picked < routed
            safe_idx = jnp.where(living, picked, 0).astype(jnp.int32)
            token_idx = (safe_idx // TOPK).astype(jnp.int32)
            chosen = tokens[token_idx]
            gate_in = jnp.dot(chosen, gate_proj[expert], preferred_element_type=jnp.float32)
            up_in = jnp.dot(chosen, up_proj[expert], preferred_element_type=jnp.float32)
            hidden = (jax.nn.silu(gate_in) * up_in).astype(jnp.bfloat16)
            result = jnp.dot(hidden, down_proj[expert], preferred_element_type=jnp.float32).astype(jnp.bfloat16)
            weighted = flat_shares[safe_idx][:, None] * result.astype(jnp.float32)
            target = jnp.where(living, token_idx, tokens.shape[0]).astype(jnp.int32)
            summed = summed.at[target].add(weighted, mode="drop")
            return summed, None
        return one_expert

    cool_list = jnp.nonzero(jnp.logical_not(hot_flag), size=experts - HOT, fill_value=0)[0].astype(jnp.int32)
    initial = jnp.zeros((tokens.shape[0], tokens.shape[1]), jnp.float32)
    summed, _ = lax.scan(make_step(CAP * devices), initial, cool_list)
    summed, _ = lax.scan(make_step(HOT_CAP * devices), summed, hot_expert)
    return summed.astype(jnp.bfloat16), served_load
```

```python
import jax
import jax.numpy as jnp
from jax import lax
from jax.experimental import pallas as pl
from jax.experimental.pallas import tpu as pltpu
from jax.sharding import Mesh
from jax.sharding import PartitionSpec as P


BF16 = jnp.bfloat16
F32 = jnp.float32
I32 = jnp.int32

D = 2048
FF = 768
TOK = 128
TOPK = 8
CHIPS = 64
COLS = 32
ROWS = CHIPS * 8
THIRD = 512
MAIN = 3 * THIRD
WIDE = 2 * D + MAIN
SENT = WIDE + 128


def big_core(hot_row, half):
    return jnp.where((hot_row >> 1) == half, hot_row & 1, 0)


def tail_target(row, q):
    low = row & 7
    return jnp.where(low == 6, 2 * ROWS + row - 6 + q, jnp.where(low == 7, 2 * ROWS + row - 4 + q, -1))


def pack_kernel(plan_ref, ids_ref, tokens_ref, out_ref, code_ref, code_s, counts_s):
    step = pl.program_id(0)

    @pl.when(step == 0)
    def _():
        expert = lax.broadcasted_iota(I32, (128, 128), 0)
        lane = lax.broadcasted_iota(I32, (128, 128), 1)
        row = expert >> 5
        col = expert & 31
        hot_row = jnp.zeros((128, 128), I32)
        for c in range(COLS):
            hot_row = jnp.where(col == c, plan_ref[c], hot_row)
        chip8 = ((row >> 1) * COLS + col) * 8
        big = (row & 1) == big_core(hot_row, row >> 1)
        base = jnp.where(big, chip8, 2 * ROWS + chip8).astype(F32)
        jump = jnp.where(big, ROWS - 8.0, 0.0)
        ids = ids_ref[...]
        named = [(ids[k : k + 1, :] == expert) for k in range(TOPK)]
        stacked = jnp.concatenate([n.astype(F32).astype(BF16) for n in named], axis=0)
        before = jnp.concatenate([(expert < lane).astype(F32).astype(BF16), jnp.ones((128, 128), BF16)], axis=1)
        prefix = jnp.dot(stacked, before, preferred_element_type=F32)
        seen = jnp.zeros((128, 128), F32)
        codes = []
        for k in range(TOPK):
            ordinal = prefix[k * 128 : (k + 1) * 128, :128] + seen
            place = base + ordinal + jnp.where(ordinal >= 8.0, jump, 0.0)
            codes.append(jnp.sum(jnp.where(named[k], place, 0.0), axis=0, keepdims=True))
            seen = seen + prefix[k * 128 : (k + 1) * 128, 128:]
        code = jnp.concatenate(codes, axis=0).astype(I32)
        code_s[...] = code
        code_ref[...] = code
        counts_s[...] = jnp.transpose(seen).astype(BF16)

    row = lax.broadcasted_iota(I32, (128, 128), 0) + step * 128
    code = code_s[...]

    def chosen(target):
        hit = code[0:1, :] == target
        for k in range(1, TOPK):
            hit = hit | (code[k : k + 1, :] == target)
        return hit.astype(F32).astype(BF16)

    tokens = tokens_ref[...]
    planes = jnp.concatenate([chosen(row), chosen(row + ROWS)], axis=0)
    picked = jnp.dot(planes, tokens, preferred_element_type=F32).astype(BF16)
    out_ref[:, :D] = picked[:128]
    out_ref[:, D : 2 * D] = picked[128:]
    main = chosen(row + 2 * ROWS)
    for q in range(3):
        both = jnp.concatenate([main, chosen(tail_target(row, q))], axis=1)
        source = jnp.concatenate([tokens[:, q * THIRD : (q + 1) * THIRD], tokens[:, MAIN:]], axis=0)
        at = 2 * D + q * THIRD
        out_ref[:, at : at + THIRD] = jnp.dot(both, source, preferred_element_type=F32).astype(BF16)
    out_ref[:, WIDE:] = counts_s[...]


def pack(hot_plan, expert_ids, tokens):
    return pl.pallas_call(
        pack_kernel,
        grid=(ROWS // 128,),
        in_specs=[
            pl.BlockSpec(memory_space=pltpu.SMEM),
            pl.BlockSpec((TOPK, TOK), lambda i: (0, 0)),
            pl.BlockSpec((TOK, D), lambda i: (0, 0)),
        ],
        out_specs=[pl.BlockSpec((128, SENT), lambda i: (i, 0)), pl.BlockSpec((TOPK, TOK), lambda i: (0, 0))],
        out_shape=[jax.ShapeDtypeStruct((ROWS, SENT), BF16), jax.ShapeDtypeStruct((TOPK, TOK), I32)],
        scratch_shapes=[pltpu.VMEM((TOPK, TOK), I32), pltpu.VMEM((128, 128), BF16)],
        compiler_params=pltpu.CompilerParams(vmem_limit_bytes=16 << 20),
        name="pack",
    )(hot_plan, expert_ids.T, tokens)


def share_mat(code, share, u):
    row = lax.broadcasted_iota(I32, (ROWS, TOK), 0)
    target = jnp.where(u < 3, row + u * ROWS, tail_target(row, u - 3))
    placed = jnp.zeros((ROWS, TOK), F32)
    for k in range(TOPK):
        placed = placed + jnp.where(code[k : k + 1, :] == target, share[k : k + 1, :], 0.0)
    placed = jnp.transpose(placed)
    high = placed.astype(BF16)
    return high, (placed - high.astype(F32)).astype(BF16)


def ffn_kernel(where_ref, plan_ref, code_ref, weight_ref, got_ref, *refs):
    own = refs[0:3]
    other = refs[3:6]
    out_ref, mats_ref = refs[6:8]
    o_s, p_s, wg_s, wu_s, wd_s, w_sem, o_sem = refs[8:]
    weights = (wg_s, wu_s, wd_s)
    me = where_ref[0]
    hot_row = plan_ref[me & 31]
    mine_is_big = big_core(hot_row, me >> 6) == ((me >> 5) & 1)

    def w_copy(source, slot, i):
        return pltpu.make_async_copy(source[i].at[0], weights[i].at[slot], w_sem.at[slot, i])

    def start(slot, i):
        first = mine_is_big if slot == 0 else jnp.logical_not(mine_is_big)

        @pl.when(first)
        def _():
            w_copy(own, slot, i).start()

        @pl.when(jnp.logical_not(first))
        def _():
            w_copy(other, slot, i).start()

    def wait(slot, i):
        w_copy(own, slot, i).wait()

    def o_copy(u):
        return pltpu.make_async_copy(
            o_s.at[u], out_ref.at[pl.ds((u % 2) * 256, 256), pl.ds(pl.multiple_of((u // 2) * D, D), D)], o_sem.at[u]
        )

    def p_copy(h):
        return pltpu.make_async_copy(p_s.at[h], out_ref.at[pl.ds(h * 256, 256), pl.ds(2 * D, MAIN)], o_sem.at[4 + h])

    row = lax.broadcasted_iota(I32, (256, 256), 0)
    col = lax.broadcasted_iota(I32, (256, 256), 1)
    same = (row >> 3) == (col >> 3)
    weight = weight_ref[...]
    share = weight / jnp.sum(weight, axis=0, keepdims=True)
    code = code_ref[...]

    def rows_of(u):
        return pl.ds(pl.multiple_of((u % 2) * 256, 256), 256)

    def shares(u):
        high, low = share_mat(code, share, u)
        mats_ref[u, :TOK, :] = high
        mats_ref[u, TOK:, :] = low

    def activate(gate_in, up_in):
        return (jax.nn.silu(gate_in) * up_in).astype(BF16)

    def dot(x, w):
        return jnp.dot(x, w, preferred_element_type=F32)

    def big_unit(u):
        x = got_ref[rows_of(u), pl.ds(pl.multiple_of((u // 2) * D, D), D)]
        hidden = activate(dot(x, wg_s[0]), dot(x, wu_s[0]))
        o_s[u] = dot(hidden, wd_s[0]).astype(BF16)
        shares(u)
        o_copy(u).start()

    def small_unit(u):
        h = u - 4
        rows = rows_of(u)
        tail = jnp.zeros((256, THIRD), F32)
        for q in range(3):
            pick = same & (((row & 7) == q) & ((col & 7) == 6) | ((row & 7) == 3 + q) & ((col & 7) == 7))
            tail = tail + dot(pick.astype(F32).astype(BF16), got_ref[rows, 2 * D + q * THIRD : 2 * D + (q + 1) * THIRD])
        tail = tail.astype(BF16)
        x = jnp.concatenate([got_ref[rows, 2 * D : 2 * D + MAIN], tail], axis=1)
        hidden = activate(dot(x, wg_s[1]), dot(x, wu_s[1]))
        result = dot(hidden, wd_s[1]).astype(BF16)
        shares(u)
        for q in range(3):
            pick = same & (((col & 7) == q) & ((row & 7) == 6) | ((col & 7) == 3 + q) & ((row & 7) == 7))
            keep = same & ((row & 7) == (col & 7)) & ((row & 7) < 6)
            both = jnp.concatenate([keep.astype(F32).astype(BF16), pick.astype(F32).astype(BF16)], axis=1)
            source = jnp.concatenate([result[:, q * THIRD : (q + 1) * THIRD], result[:, MAIN:]], axis=0)
            p_s[h, :, q * THIRD : (q + 1) * THIRD] = dot(both, source).astype(BF16)
        p_copy(h).start()

    start(0, 0)
    start(0, 1)
    wait(0, 0)
    start(0, 2)
    x = got_ref[:256, :D]
    gate_in = dot(x, wg_s[0])
    wait(0, 1)
    for i in range(3):
        start(1, i)
    hidden = activate(gate_in, dot(x, wu_s[0]))
    wait(0, 2)
    o_s[0] = dot(hidden, wd_s[0]).astype(BF16)
    shares(0)
    o_copy(0).start()
    lax.fori_loop(1, 4, lambda u, c: (big_unit(u), c)[1], 0)
    for i in range(3):
        wait(1, i)
    lax.fori_loop(4, 6, lambda u, c: (small_unit(u), c)[1], 0)
    for u in range(4):
        o_copy(u).wait()
    for h in range(2):
        p_copy(h).wait()


def ffn(where, hot_plan, code, route_weight, got, own, other):
    hbm = pl.BlockSpec(memory_space=pltpu.HBM)
    anywhere = pl.BlockSpec(memory_space=pl.ANY)
    smem = pl.BlockSpec(memory_space=pltpu.SMEM)
    vmem = pl.BlockSpec(memory_space=pltpu.VMEM)
    return pl.pallas_call(
        ffn_kernel,
        in_specs=[smem, smem, vmem, vmem, vmem] + [hbm] * 6,
        out_specs=[anywhere, vmem],
        out_shape=[jax.ShapeDtypeStruct((ROWS, WIDE), BF16), jax.ShapeDtypeStruct((6, 2 * TOK, ROWS), BF16)],
        scratch_shapes=[
            pltpu.VMEM((4, 256, D), BF16),
            pltpu.VMEM((2, 256, MAIN), BF16),
            pltpu.VMEM((2, D, FF), BF16),
            pltpu.VMEM((2, D, FF), BF16),
            pltpu.VMEM((2, FF, D), BF16),
            pltpu.SemaphoreType.DMA((2, 3)),
            pltpu.SemaphoreType.DMA((6,)),
        ],
        compiler_params=pltpu.CompilerParams(vmem_limit_bytes=FFN_VMEM),
        name="ffn",
    )(where, hot_plan, code, route_weight.T, got, *own, *other)


def combine_kernel(where_ref, plan_ref, mine_ref, theirs_ref, mats_ref, back_ref, out_ref, served_ref):
    def part(i, j):
        return jnp.dot(mats_ref[i], back_ref[:, j * THIRD : (j + 1) * THIRD], preferred_element_type=F32)

    for n in range(4):
        total = part(0, n) + part(1, 4 + n)
        if n < 3:
            total = total + part(2, 8 + n)
        else:
            for q in range(3):
                total = total + part(3 + q, 8 + q)
        out_ref[:, n * THIRD : (n + 1) * THIRD] = (total[:TOK] + total[TOK:]).astype(BF16)

    expert = lax.broadcasted_iota(I32, (1, 128), 1)
    hot_row = jnp.zeros((1, 128), I32)
    for c in range(COLS):
        hot_row = jnp.where((expert & 31) == c, plan_ref[c], hot_row)
    hot = hot_row == (expert >> 5)
    mine = mine_ref[...]
    theirs = theirs_ref[...]
    low = ((where_ref[0] >> 5) & 1) == 0
    even = jnp.where(low, mine, theirs)
    odd = jnp.where(low, theirs, mine)
    counts = jnp.concatenate([even[0:1], odd[0:1], even[1:2], odd[1:2]], axis=0)
    kept = jnp.where(hot, counts, 0.0)
    folded = kept
    for turn in range(1, 4):
        folded = folded + jnp.concatenate([kept[:, 32 * turn :], kept[:, : 32 * turn]], axis=1)
    served = jnp.where(hot, 0.0, jnp.sum(counts, axis=0, keepdims=True))
    for r in range(4):
        served = served + jnp.where((expert >> 5) == r, folded[r : r + 1], 0.0)
    served_ref[...] = served / F32(TOK * TOPK)


def combine(where, hot_plan, mine, theirs, mats, back):
    smem = pl.BlockSpec(memory_space=pltpu.SMEM)
    vmem = pl.BlockSpec(memory_space=pltpu.VMEM)
    return pl.pallas_call(
        combine_kernel,
        in_specs=[smem, smem, vmem, vmem, vmem, vmem],
        out_specs=[vmem, vmem],
        out_shape=[jax.ShapeDtypeStruct((TOK, D), BF16), jax.ShapeDtypeStruct((1, 128), F32)],
        compiler_params=pltpu.CompilerParams(vmem_limit_bytes=16 << 20),
        name="combine",
    )(where, hot_plan, mine, theirs, mats, back)


def swap_cores(array):
    return lax.ppermute(array, "d", [(i, i ^ COLS) for i in range(128)])


def across_chips(array):
    groups = [[half * 64 + core * 32 + c for half in range(2) for c in range(COLS)] for core in range(2)]
    width = array.shape[1]
    blocks = array.reshape(CHIPS, 8, width)
    moved = lax.all_to_all(blocks, "d", split_axis=0, concat_axis=0, axis_index_groups=groups, tiled=True)
    return moved.reshape(ROWS, width)


def local(tokens, expert_ids, route_weight, hot_plan, gate_proj, up_proj, down_proj):
    me = lax.axis_index("d").reshape(1).astype(I32)
    own = (gate_proj, up_proj, down_proj)
    other = []
    for w in own:
        other.append(swap_cores(w))
    sent, code = pack(hot_plan, expert_ids, tokens)
    got = across_chips(sent)
    mine = jnp.sum(got[:, WIDE:].astype(F32).reshape(2, COLS * 8, 128), axis=1) * 0.125
    theirs = swap_cores(mine)
    done, mats = ffn(me, hot_plan, code, route_weight, got, own, other)
    back = across_chips(done)
    layer_out, served_load = combine(me, hot_plan, mine, theirs, mats, back)
    return layer_out, served_load.reshape(128)


FFN_VMEM = 36 << 20


def solution(mesh):
    flat = Mesh(mesh.devices.reshape(128), ("d",))
    placed = (P("d", None), P("d", None), P("d", None), P(), P("d", None, None), P("d", None, None), P("d", None, None))
    return jax.shard_map(local, mesh=flat, in_specs=placed, out_specs=(P("d", None), P()), check_vma=False)
```

```python
import jax
import jax.numpy as jnp
from jax import lax
from jax.experimental import pallas as pl
from jax.experimental.pallas import tpu as pltpu
from jax.sharding import Mesh
from jax.sharding import PartitionSpec as P


BF16 = jnp.bfloat16
F32 = jnp.float32
I32 = jnp.int32

D = 2048
FF = 768
TOK = 128
TOPK = 8
CHIPS = 64
COLS = 32
ROWS = CHIPS * 8
THIRD = 512
MAIN = 3 * THIRD
WIDE = 2 * D + MAIN
SENT = WIDE + 128


def big_core(hot_row, half):
    return jnp.where((hot_row >> 1) == half, hot_row & 1, 0)


def tail_target(row, q):
    low = row & 7
    return jnp.where(low == 6, 2 * ROWS + row - 6 + q, jnp.where(low == 7, 2 * ROWS + row - 4 + q, -1))


def in_hbm(array):
    return pltpu.with_memory_space_constraint(array, pltpu.HBM)


def in_vmem(array):
    return pltpu.with_memory_space_constraint(array, pltpu.VMEM)


def tail_pick(row, col, q):
    same = (row >> 3) == (col >> 3)
    pick = same & (((row & 7) == 6) & ((col & 7) == q) | ((row & 7) == 7) & ((col & 7) == 3 + q))
    return pick.astype(F32).astype(BF16)


def pack_kernel(where_ref, plan_ref, ids_ref, weight_ref, tokens_ref, gate_ref, up_ref, out_ref, code_ref, share_ref, gate_v, up_v, sem):
    keeps = [pltpu.make_async_copy(gate_ref, gate_v, sem.at[0]), pltpu.make_async_copy(up_ref, up_v, sem.at[1])]
    for keep in keeps:
        keep.start()
    me = where_ref[0]
    mine_is_big = big_core(plan_ref[me & 31], me >> 6) == ((me >> 5) & 1)
    weight = weight_ref[...]
    share_ref[:TOPK, :] = weight / jnp.sum(weight, axis=0, keepdims=True)
    lane8 = lax.broadcasted_iota(I32, (TOPK, TOK), 1)
    row8 = lax.broadcasted_iota(I32, (TOPK, TOK), 0)
    hot8 = jnp.zeros((TOPK, TOK), I32)
    for c in range(COLS):
        hot8 = jnp.where((lane8 & 31) == c, plan_ref[c], hot8)
    flags = jnp.where(row8 == 0, mine_is_big.astype(I32), jnp.where(row8 == 1, (me >> 5) & 1, (hot8 == (lane8 >> 5)).astype(I32)))
    share_ref[TOPK:, :] = flags.astype(F32)
    expert = lax.broadcasted_iota(I32, (128, 128), 0)
    lane = lax.broadcasted_iota(I32, (128, 128), 1)
    row = expert >> 5
    col = expert & 31
    hot_row = jnp.zeros((128, 128), I32)
    for c in range(COLS):
        hot_row = jnp.where(col == c, plan_ref[c], hot_row)
    chip8 = ((row >> 1) * COLS + col) * 8
    big = (row & 1) == big_core(hot_row, row >> 1)
    base = jnp.where(big, chip8, 2 * ROWS + chip8).astype(F32)
    jump = jnp.where(big, ROWS - 8.0, 0.0)
    ids = ids_ref[...]
    named = [(ids[k : k + 1, :] == expert) for k in range(TOPK)]
    stacked = jnp.concatenate([n.astype(F32).astype(BF16) for n in named], axis=0)
    before = jnp.concatenate([(expert < lane).astype(F32).astype(BF16), jnp.ones((128, 128), BF16)], axis=1)
    prefix = jnp.dot(stacked, before, preferred_element_type=F32)
    seen = jnp.zeros((128, 128), F32)
    codes = []
    for k in range(TOPK):
        ordinal = prefix[k * 128 : (k + 1) * 128, :128] + seen
        place = base + ordinal + jnp.where(ordinal >= 8.0, jump, 0.0)
        codes.append(jnp.sum(jnp.where(named[k], place, 0.0), axis=0, keepdims=True))
        seen = seen + prefix[k * 128 : (k + 1) * 128, 128:]
    code = jnp.concatenate(codes, axis=0).astype(I32)
    code_ref[...] = code
    counts = jnp.transpose(seen).astype(BF16)

    code_f = code.astype(F32)

    def chosen(start, target):
        near = jnp.clip(code_f - start, -1.0, 128.0)
        hit = jnp.zeros((128, 128), BF16)
        for k in range(TOPK):
            one = jnp.broadcast_to(near[k : k + 1, :], (16, TOK)).astype(BF16)
            hit = jnp.where(jnp.concatenate([one] * 8, axis=0) == target, jnp.ones((), BF16), hit)
        return hit

    local_row = expert.astype(F32).astype(BF16)
    low = expert & 7
    tails = [
        jnp.where(low == 6, expert - 6 + q, jnp.where(low == 7, expert - 4 + q, -2)).astype(F32).astype(BF16) for q in range(3)
    ]

    tokens = tokens_ref[...]

    def step(i, carry):
        start = (i * 128).astype(F32)
        rows = pl.ds(pl.multiple_of(i * 128, 128), 128)
        planes = jnp.concatenate([chosen(start, local_row), chosen(start + ROWS, local_row)], axis=0)
        picked = jnp.dot(planes, tokens, preferred_element_type=F32).astype(BF16)
        out_ref[rows, :D] = picked[:128]
        out_ref[rows, D : 2 * D] = picked[128:]
        main = chosen(start + 2 * ROWS, local_row)
        for q in range(3):
            both = jnp.concatenate([main, chosen(start + 2 * ROWS, tails[q])], axis=1)
            source = jnp.concatenate([tokens[:, q * THIRD : (q + 1) * THIRD], tokens[:, MAIN:]], axis=0)
            at = 2 * D + q * THIRD
            out_ref[rows, at : at + THIRD] = jnp.dot(both, source, preferred_element_type=F32).astype(BF16)
        out_ref[rows, WIDE:] = counts
        return carry

    lax.fori_loop(0, ROWS // 128, step, 0)
    for keep in keeps:
        keep.wait()


def pack(where, hot_plan, expert_ids, route_weight, tokens, gate_proj, up_proj):
    smem = pl.BlockSpec(memory_space=pltpu.SMEM)
    vmem = pl.BlockSpec(memory_space=pltpu.VMEM)
    hbm = pl.BlockSpec(memory_space=pltpu.HBM)
    return pl.pallas_call(
        pack_kernel,
        in_specs=[smem, smem, vmem, vmem, vmem, hbm, hbm],
        out_specs=[vmem] * 5,
        out_shape=[
            pltpu.VMEM((ROWS, SENT), BF16),
            pltpu.VMEM((TOPK, TOK), I32),
            pltpu.VMEM((2 * TOPK, TOK), F32),
            pltpu.VMEM((1, D, FF), BF16),
            pltpu.VMEM((1, D, FF), BF16),
        ],
        scratch_shapes=[pltpu.SemaphoreType.DMA((2,))],
        compiler_params=pltpu.CompilerParams(vmem_limit_bytes=FFN_VMEM),
        name="pack",
    )(where, in_hbm(hot_plan), in_hbm(expert_ids.T), in_hbm(route_weight.T), in_hbm(tokens), in_hbm(gate_proj), in_hbm(up_proj))


def tally_kernel(got_ref, out_ref):
    for half in range(2):
        counts = got_ref[half * 256 : (half + 1) * 256, WIDE:].astype(F32)
        out_ref[half : half + 1, :] = jnp.sum(counts, axis=0, keepdims=True) * 0.125


def tally(got):
    vmem = pl.BlockSpec(memory_space=pltpu.VMEM)
    return pl.pallas_call(
        tally_kernel,
        in_specs=[vmem],
        out_specs=vmem,
        out_shape=jax.ShapeDtypeStruct((2, 128), F32),
        compiler_params=pltpu.CompilerParams(vmem_limit_bytes=FFN_VMEM),
        name="tally",
    )(in_vmem(got))


def share_mat(code, share, u):
    row = lax.broadcasted_iota(I32, (ROWS, TOK), 0)
    target = jnp.where(u < 3, row + u * ROWS, tail_target(row, u - 3))
    placed = jnp.zeros((ROWS, TOK), F32)
    for k in range(TOPK):
        placed = placed + jnp.where(code[k : k + 1, :] == target, share[k : k + 1, :], 0.0)
    placed = jnp.transpose(placed)
    high = placed.astype(BF16)
    return high, (placed - high.astype(F32)).astype(BF16)


def ffn_kernel(code_ref, share_ref, got_ref, *refs):
    own = refs[0:3]
    other = refs[3:6]
    out_ref, mats_ref = refs[6:8]
    down_s, gate_s, up_s, other_down_s, pick_s, w_sem = refs[8:]
    mine = (own[0], own[1], down_s)
    theirs = (gate_s, up_s, other_down_s)
    mine_is_big = jnp.max(share_ref[TOPK : TOPK + 1, :]) > 0.5

    fetches = [
        pltpu.make_async_copy(source, target, w_sem.at[i])
        for i, (source, target) in enumerate(
            [(own[2], down_s), (other[0], gate_s), (other[1], up_s), (other[2], other_down_s)]
        )
    ]
    fetches[0].start()

    code = code_ref[...]
    share = share_ref[:TOPK, :]

    def shares(u):
        high, low = share_mat(code, share, u)
        mats_ref[u, :TOK, :] = high
        mats_ref[u, TOK:, :] = low

    def activate(gate_in, up_in):
        return (jax.nn.silu(gate_in) * up_in).astype(BF16)

    def dot(x, w):
        return jnp.dot(x, w, preferred_element_type=F32)

    def big_unit(u, w, wait=None):
        lanes = pl.ds(pl.multiple_of(u * D, D), D)
        x = got_ref[:, lanes]
        hidden = activate(dot(x, w[0][0]), dot(x, w[1][0]))
        if wait is not None:
            wait()
        out_ref[:, lanes] = dot(hidden, w[2][0]).astype(BF16)
        shares(2 * u)
        shares(2 * u + 1)

    def small_unit(w, wait=None):
        parts = []
        for h in range(2):
            rows = slice(h * 256, (h + 1) * 256)
            tail = jnp.zeros((256, THIRD), F32)
            for q in range(3):
                tail = tail + dot(pick_s[q], got_ref[rows, 2 * D + q * THIRD : 2 * D + (q + 1) * THIRD])
            parts.append(tail.astype(BF16))
        x = jnp.concatenate([got_ref[:, 2 * D : 2 * D + MAIN], jnp.concatenate(parts, axis=0)], axis=1)
        hidden = activate(dot(x, w[0][0]), dot(x, w[1][0]))
        if wait is not None:
            wait()
        result = dot(hidden, w[2][0]).astype(BF16)
        shares(4)
        shares(5)
        main_row = (lax.broadcasted_iota(I32, (256, THIRD), 0) & 7) < 6
        for h in range(2):
            rows = slice(h * 256, (h + 1) * 256)
            for q in range(3):
                moved = dot(pick_s[3 + q], result[rows, MAIN:])
                main = result[rows, q * THIRD : (q + 1) * THIRD].astype(F32)
                out_ref[rows, 2 * D + q * THIRD : 2 * D + (q + 1) * THIRD] = jnp.where(main_row, main, moved).astype(BF16)

    row = lax.broadcasted_iota(I32, (256, 256), 0)
    col = lax.broadcasted_iota(I32, (256, 256), 1)
    for q in range(3):
        pick_s[q] = tail_pick(col, row, q)
        pick_s[3 + q] = tail_pick(row, col, q)

    def own_down():
        fetches[0].wait()
        for fetch in fetches[1:]:
            fetch.start()

    def rest():
        for fetch in fetches[1:]:
            fetch.wait()

    @pl.when(mine_is_big)
    def _():
        big_unit(0, mine, own_down)
        big_unit(1, mine)
        rest()
        small_unit(theirs)

    @pl.when(jnp.logical_not(mine_is_big))
    def _():
        small_unit(mine, own_down)
        rest()
        lax.fori_loop(0, 2, lambda u, c: (big_unit(u, theirs), c)[1], 0)


def ffn(code, share, got, own, other):
    hbm = pl.BlockSpec(memory_space=pltpu.HBM)
    smem = pl.BlockSpec(memory_space=pltpu.SMEM)
    vmem = pl.BlockSpec(memory_space=pltpu.VMEM)
    return pl.pallas_call(
        ffn_kernel,
        in_specs=[vmem] * 5 + [hbm] * 4,
        out_specs=[vmem, vmem],
        out_shape=[pltpu.VMEM((ROWS, WIDE), BF16), pltpu.VMEM((6, 2 * TOK, ROWS), BF16)],
        scratch_shapes=[
            pltpu.VMEM((1, FF, D), BF16),
            pltpu.VMEM((1, D, FF), BF16),
            pltpu.VMEM((1, D, FF), BF16),
            pltpu.VMEM((1, FF, D), BF16),
            pltpu.VMEM((6, 256, 256), BF16),
            pltpu.SemaphoreType.DMA((4,)),
        ],
        compiler_params=pltpu.CompilerParams(vmem_limit_bytes=FFN_VMEM),
        name="ffn",
    )(in_vmem(code), in_vmem(share), in_vmem(got), in_vmem(own[0]), in_vmem(own[1]), in_hbm(own[2]), *other)


def combine_kernel(share_ref, mine_ref, theirs_ref, mats_ref, back_ref, out_ref, served_ref):
    def part(i, j):
        return jnp.dot(mats_ref[i], back_ref[:, j * THIRD : (j + 1) * THIRD], preferred_element_type=F32)

    for n in range(4):
        total = part(0, n) + part(1, 4 + n)
        if n < 3:
            total = total + part(2, 8 + n)
        else:
            for q in range(3):
                total = total + part(3 + q, 8 + q)
        out_ref[:, n * THIRD : (n + 1) * THIRD] = (total[:TOK] + total[TOK:]).astype(BF16)

    expert = lax.broadcasted_iota(I32, (1, 128), 1)
    hot = share_ref[TOPK + 2 : TOPK + 3, :] > 0.5
    mine = mine_ref[...]
    theirs = theirs_ref[...]
    low = share_ref[TOPK + 1 : TOPK + 2, :] < 0.5
    even = jnp.where(low, mine, theirs)
    odd = jnp.where(low, theirs, mine)
    counts = jnp.concatenate([even[0:1], odd[0:1], even[1:2], odd[1:2]], axis=0)
    kept = jnp.where(hot, counts, 0.0)
    folded = kept
    for turn in range(1, 4):
        folded = folded + jnp.concatenate([kept[:, 32 * turn :], kept[:, : 32 * turn]], axis=1)
    served = jnp.where(hot, 0.0, jnp.sum(counts, axis=0, keepdims=True))
    for r in range(4):
        served = served + jnp.where((expert >> 5) == r, folded[r : r + 1], 0.0)
    served_ref[...] = served / F32(TOK * TOPK)


def combine(share, mine, theirs, mats, back):
    vmem = pl.BlockSpec(memory_space=pltpu.VMEM)
    return pl.pallas_call(
        combine_kernel,
        in_specs=[vmem] * 5,
        out_specs=[vmem, vmem],
        out_shape=[jax.ShapeDtypeStruct((TOK, D), BF16), jax.ShapeDtypeStruct((1, 128), F32)],
        compiler_params=pltpu.CompilerParams(vmem_limit_bytes=FFN_VMEM),
        name="combine",
    )(in_vmem(share), mine, theirs, in_vmem(mats), in_vmem(back))


def swap_cores(array):
    return lax.ppermute(array, "d", [(i, i ^ COLS) for i in range(128)])


def across_chips(array):
    groups = [[half * 64 + core * 32 + c for half in range(2) for c in range(COLS)] for core in range(2)]
    width = array.shape[1]
    blocks = array.reshape(CHIPS, 8, width)
    moved = lax.all_to_all(blocks, "d", split_axis=0, concat_axis=0, axis_index_groups=groups, tiled=True)
    return moved.reshape(ROWS, width)


def local(tokens, expert_ids, route_weight, hot_plan, gate_proj, up_proj, down_proj):
    me = lax.axis_index("d").reshape(1).astype(I32)
    own = (gate_proj, up_proj, down_proj)
    other = []
    for w in own:
        other.append(swap_cores(w))
    sent, code, share, gate_v, up_v = pack(me, hot_plan, expert_ids, route_weight, tokens, gate_proj, up_proj)
    got = across_chips(sent)
    mine = tally(got)
    theirs = swap_cores(mine)
    done, mats = ffn(code, share, got, (gate_v, up_v, down_proj), other)
    back = across_chips(done)
    layer_out, served_load = combine(share, mine, theirs, mats, back)
    return layer_out, served_load.reshape(128)


FFN_VMEM = 30 << 20


def solution(mesh):
    flat = Mesh(mesh.devices.reshape(128), ("d",))
    placed = (P("d", None), P("d", None), P("d", None), P(), P("d", None, None), P("d", None, None), P("d", None, None))
    return jax.shard_map(local, mesh=flat, in_specs=placed, out_specs=(P("d", None), P()), check_vma=False)
```
